32 devices in a mesh: sub: 8 (over z, x), scen: 4 (over y, core).
Axes of the slice: x: 2, y: 2, z: 4, core: 2. Of those that a mesh axis runs over, the one named last changes fastest.
Arguments:
- internal_inverse: bfloat16 [32, 1024, 1024], P('sub', 'scen')
- schur_inverse: bfloat16 [512, 512], P('sub')
- port_nodes: int32 [32, 16], P('sub'), may hold values from 0 to 1023, as said below
- turbine_count: int32 [8], P('sub'), may hold values from 1 to 4, as said below
- partner_port: int32 [512], P('sub'), may hold values from 0 to 511, as said below
- cable_delay: int32 [512], P('sub'), may hold values from 2 to 4, as said below
- history_w: bfloat16 [4, 256, 512], P(None, 'scen', 'sub'), may hold values from -6 to 6
- node_state: float32 [256, 32, 1024], P('scen', 'sub'), may hold values from -6 to 6
- node_gain: float32 [32, 1024], P('sub'), may hold values from 0.02 to 0.3
- stroke_node: int32 [256], P('scen'), may hold values from 0 to 32767, as said below
- stroke_amp: float32 [256], P('scen'), may hold values from 3 to 30
Outputs:
- node_voltage: bfloat16 [256, 32, 1024], P('scen', 'sub')
- cable_waves: bfloat16 [3, 256, 512], P(None, 'scen', 'sub')
The draws below stay inside these ranges and needn't reach their ends.
Inputs may be any that keep to these rules, and one draw needn't show every extreme that they name: `port_nodes`: the 16 nodes named for one slot are distinct. `turbine_count`: the turbines of one index of sub fill its first slots; the busiest hold all 4. `partner_port`: a cable joins two ports that name each other, of a turbine and the next turbine in slot order (the next used slot, on the same or the next index of sub); a port that names itself has no cable. `cable_delay`: both ends of a cable carry the same delay. `stroke_node`: slot times 1024 plus local node; a stroke on an empty slot injects nothing.
All inputs are finite; a program needn't handle non-finite values.
Results may differ from the reference program's by a relative error of at most 0.004.
The reference program's roundings to bfloat16 on the way (of `port_rows`, `injected` and `link_half`) count: a program that leaves them out, or rounds other values in their place, can miss the bound.
Values may be sent and summed in bfloat16 or wider, within the bound.
A program may use at most 64 MiB of HBM per device.

```python
import math
import jax
import jax.numpy as jnp
from jax import lax

NODES = 1024
PORTS = 16
SLOTS = 4
SCEN_DEV = 64
STEPS = 3
MAXDELAY = 4
SCEN = 256
TURB_SLOTS = 32
IFACE = 512
N_SUB = 8
N_SCEN = 4


def slot_counts(key):
    key_one, key_two, key_three, key_four = jax.random.split(jax.random.fold_in(key, 101), 4)
    first_draw = jax.random.randint(key_one, (N_SUB,), 0, SLOTS)
    second_draw = jax.random.randint(key_two, (N_SUB,), 0, SLOTS)
    counts = 1 + first_draw * second_draw // (SLOTS - 1)
    full_device = jax.random.randint(key_three, (), 0, N_SUB)
    second = (full_device + 1 + jax.random.randint(key_four, (), 0, N_SUB - 1)) % N_SUB
    counts = counts.at[full_device].set(SLOTS).at[second].set(1)
    return counts.astype(jnp.int32)


def cable_layout(key):
    counts = slot_counts(key)
    slot_total = N_SUB * SLOTS
    slot_ids = jnp.arange(slot_total, dtype=jnp.int32)
    occupied = slot_ids % SLOTS < counts[slot_ids // SLOTS]
    candidate = jnp.where(occupied, slot_ids, slot_total)
    following = lax.cummin(candidate, axis=0, reverse=True)
    next_slot = jnp.concatenate([following[1:], jnp.full((1,), slot_total, jnp.int32)])
    linked = occupied & (next_slot < slot_total)
    half_ports = PORTS // 2
    key_ports, key_delay = jax.random.split(jax.random.fold_in(key, 102))
    shuffle = jax.vmap(lambda single: jax.random.permutation(single, half_ports))(jax.random.split(key_ports, slot_total)).astype(jnp.int32)
    port_offset = jnp.arange(half_ports, dtype=jnp.int32)
    down_port = slot_ids[:, None] * PORTS + half_ports + port_offset[None, :]
    up_port = next_slot[:, None] * PORTS + shuffle
    sink_index = slot_total * PORTS
    down_pos = jnp.where(linked[:, None], down_port, sink_index).reshape(-1)
    up_pos = jnp.where(linked[:, None], up_port, sink_index).reshape(-1)
    delays = jax.random.randint(key_delay, (slot_total, half_ports), 2, MAXDELAY + 1).astype(jnp.int32)
    delays = delays.at[0, 0].set(2).at[0, 1].set(MAXDELAY).reshape(-1)
    identity_map = jnp.arange(sink_index + 1, dtype=jnp.int32)
    partner = identity_map.at[down_pos].set(up_port.reshape(-1)).at[up_pos].set(down_port.reshape(-1))[:sink_index]
    delay_map = jnp.full((sink_index + 1,), 2, jnp.int32).at[down_pos].set(delays).at[up_pos].set(delays)[:sink_index]
    return (partner, delay_map)


def draw_turbine_count(key, part):
    return slot_counts(key)


def draw_partner_port(key, part):
    return cable_layout(key)[0]


def draw_cable_delay(key, part):
    return cable_layout(key)[1]


def draw_port_nodes(key, part):
    slot_keys = jax.random.split(jax.random.fold_in(key, 103), N_SUB * SLOTS)
    chosen = jax.vmap(lambda single: jax.random.permutation(single, NODES - 2)[:PORTS])(slot_keys).astype(jnp.int32) + 1
    return chosen.at[0, 0].set(0).at[0, 1].set(NODES - 1)


def draw_stroke_node(key, part):
    picks = jax.random.randint(jax.random.fold_in(key, 104), (SCEN_DEV * N_SCEN,), 0, N_SUB * SLOTS * NODES).astype(jnp.int32)
    return picks.at[0].set(0).at[1].set(N_SUB * SLOTS * NODES - 1)


def draw_internal_inverse(key, part):
    slot_keys = jax.random.split(jax.random.fold_in(key, 201), N_SUB * SLOTS)
    identity = (jnp.arange(NODES)[:, None] == jnp.arange(NODES)[None, :]).astype(jnp.float32)

    def one_slot(single):
        key_rough, key_diag = jax.random.split(single)
        roughness = jax.random.normal(key_rough, (NODES, NODES), jnp.float32)
        diagonal = jnp.exp(jax.random.uniform(key_diag, (NODES,), jnp.float32, math.log(0.3), math.log(1.0)))
        return (roughness * (0.5 / math.sqrt(NODES)) + identity * diagonal[:, None]).astype(jnp.bfloat16)
    return lax.map(one_slot, slot_keys)


def draw_schur_inverse(key, part):
    size_total = N_SUB * SLOTS * PORTS
    key_rough, key_diag = jax.random.split(jax.random.fold_in(key, 202))
    identity = (jnp.arange(size_total)[:, None] == jnp.arange(size_total)[None, :]).astype(jnp.float32)
    roughness = jax.random.normal(key_rough, (size_total, size_total), jnp.float32)
    diagonal = jnp.exp(jax.random.uniform(key_diag, (size_total,), jnp.float32, math.log(1.0), math.log(2.0)))
    return (roughness * (2.0 / math.sqrt(size_total)) + identity * diagonal[:, None]).astype(jnp.bfloat16)


def level_of(rng, extent, shards, low, high):
    def one(dim, parts):
        draws = jax.random.uniform(jax.random.fold_in(jax.random.fold_in(rng, 6), dim), (parts,), jnp.float32, low / len(shards), high / len(shards))
        return jnp.repeat(jnp.exp(draws), extent[dim] // parts).reshape((-1,) + (1,) * (len(extent) - dim - 1))

    loudness = one(*shards[0])
    for cut in shards[1:]:
        loudness = loudness * one(*cut)
    return loudness


def bell_draw(own_key, dims, spread, reach, cuts=(), held_as=jnp.bfloat16):
    gain = level_of(own_key, dims, cuts, -0.22, 0.18) if cuts else 1.0
    entries = jax.random.normal(own_key, dims, jnp.float32) * spread * gain
    return jnp.minimum(jnp.maximum(entries, -reach), reach).astype(held_as)


def setup_inputs(seed: int = 0) -> dict:
    arg_keys = jax.random.split(jax.random.key(seed), 12)
    return {
        "internal_inverse": draw_internal_inverse(jax.random.fold_in(arg_keys[11], 71), 0),
        "schur_inverse": draw_schur_inverse(jax.random.fold_in(arg_keys[11], 71), 0),
        "port_nodes": draw_port_nodes(jax.random.fold_in(arg_keys[11], 71), 0),
        "turbine_count": draw_turbine_count(jax.random.fold_in(arg_keys[11], 71), 0),
        "partner_port": draw_partner_port(jax.random.fold_in(arg_keys[11], 71), 0),
        "cable_delay": draw_cable_delay(jax.random.fold_in(arg_keys[11], 71), 0),
        "history_w": bell_draw(arg_keys[6], (MAXDELAY, SCEN, IFACE), 1.0, 6.0, ((1, 4), (2, 8))),
        "node_state": bell_draw(arg_keys[7], (SCEN, TURB_SLOTS, NODES), 1.0, 6.0, ((0, 4), (1, 8)), jnp.float32),
        "node_gain": jnp.clip(jnp.exp(math.log(0.3) - 2.7080503 * jax.random.uniform(arg_keys[8], (TURB_SLOTS, NODES), jnp.float32) ** level_of(arg_keys[8], (TURB_SLOTS, NODES), ((0, 8),), -0.2, 0.2)), 0.02, 0.3),
        "stroke_node": draw_stroke_node(jax.random.fold_in(arg_keys[11], 71), 0),
        "stroke_amp": jnp.clip(jnp.exp(math.log(30.0) - 2.3025851 * jax.random.uniform(arg_keys[10], (SCEN,), jnp.float32) ** level_of(arg_keys[10], (SCEN,), ((0, 4),), -0.2, 0.2)), 3.0, 30.0),
    }


def contract(injected, internal_inverse):
    def one_slot(operands):
        return jnp.dot(operands[0].astype(jnp.float32), operands[1].astype(jnp.float32), precision=lax.Precision.HIGHEST)
    mapped = lax.map(one_slot, (jnp.swapaxes(injected, 0, 1), internal_inverse))
    return jnp.swapaxes(mapped, 0, 1)


def reference(internal_inverse, schur_inverse, port_nodes, turbine_count, partner_port, cable_delay, history_w, node_state, node_gain, stroke_node, stroke_amp):
    slot_ids = jnp.arange(N_SUB * SLOTS, dtype=jnp.int32)
    slot_used = ((slot_ids % SLOTS) < turbine_count[slot_ids // SLOTS]).astype(jnp.float32)
    port_used = jnp.repeat(slot_used, PORTS)
    port_rows = jnp.take_along_axis(internal_inverse, port_nodes[:, :, None], axis=1)
    node_range = jnp.arange(NODES, dtype=jnp.int32)
    port_hot = (port_nodes[:, :, None] == node_range[None, None, :]).astype(jnp.float32)
    node_ids = slot_ids[:, None] * NODES + node_range[None, :]
    stroke_hot = stroke_node[:, None, None] == node_ids[None]
    own_ports = jnp.arange(IFACE, dtype=jnp.int32)
    paired = (partner_port != own_ports).astype(jnp.float32)
    hist_cols = jnp.take(history_w, partner_port, axis=2).astype(jnp.float32)
    schur_wide = schur_inverse.astype(jnp.float32)
    fresh_cols = jnp.zeros((SCEN, IFACE), jnp.float32)
    companion = node_state
    wave_list = []
    voltage = jnp.zeros((SCEN, N_SUB * SLOTS, NODES), jnp.float32)
    for step_index in range(STEPS):
        time_now = step_index + 1
        lag_time = time_now - cable_delay
        picked = jnp.zeros((SCEN, IFACE), jnp.float32)
        for delay_back in range(MAXDELAY):
            picked = picked + jnp.where((lag_time == -delay_back)[None, :], hist_cols[delay_back], 0.0)
        picked = picked + jnp.where((lag_time == 1)[None, :], fresh_cols, 0.0)
        cable_in = -picked * paired[None, :]
        inject = jnp.einsum("sgp,gpn->sgn", cable_in.reshape(SCEN, N_SUB * SLOTS, PORTS), port_hot, precision=lax.Precision.HIGHEST)
        wave_value = math.exp(-0.3 * time_now) - math.exp(-2.0 * time_now)
        strike = jnp.where(stroke_hot, (stroke_amp * wave_value)[:, None, None], 0.0)
        injected = (slot_used[None, :, None] * (companion + strike + inject)).astype(jnp.bfloat16)
        opened = contract(injected, internal_inverse)
        port_open = jnp.take_along_axis(opened, port_nodes[None], axis=2).reshape(SCEN, IFACE)
        link_current = jnp.dot(port_open, schur_wide.T, precision=lax.Precision.HIGHEST)
        link_half = link_current.astype(jnp.bfloat16).reshape(SCEN, N_SUB * SLOTS, PORTS)
        correction = jnp.einsum("sgp,gpn->sgn", link_half.astype(jnp.float32), port_rows.astype(jnp.float32), precision=lax.Precision.HIGHEST)
        voltage = slot_used[None, :, None] * (opened - correction)
        companion = -companion - 2.0 * node_gain[None] * voltage
        port_volt = jnp.take_along_axis(voltage, port_nodes[None], axis=2).reshape(SCEN, IFACE)
        outgoing = (port_used[None, :] * (0.5 * port_volt + cable_in)).astype(jnp.bfloat16)
        wave_list.append(outgoing)
        if step_index == 0:
            fresh_cols = jnp.take(outgoing, partner_port, axis=1).astype(jnp.float32)
    return voltage.astype(jnp.bfloat16), jnp.stack(wave_list)
```

```python
import functools
import math

import jax
import jax.numpy as jnp
from jax import lax
from jax.experimental import pallas as pl
from jax.experimental.pallas import tpu as pltpu
from jax.sharding import PartitionSpec as P

STEPS = 3
SPLIT = 2
F32 = jnp.float32
BF16 = jnp.bfloat16
MESH = pl.DeviceIdType.MESH


def dot(left, right):
    return jnp.dot(left, right, preferred_element_type=F32)


def dot_t(left, right):
    return lax.dot_general(left, right, (((1,), (1,)), ((), ())), preferred_element_type=F32)


def kernel(
    n_sub,
    inv,
    schur,
    port_nodes,
    turbine_count,
    partner,
    delay,
    hist,
    node_state,
    gain,
    stroke_node,
    stroke_amp,
    volt_out,
    wave_out,
    full,
    state_in,
    companion,
    opened,
    lhs,
    prow,
    pct,
    pcb,
    gbuf,
    sbuf,
    hbuf,
    fbuf,
    own_sem,
    state_sem,
    w_send,
    w_recv,
    pc_send,
    pc_recv,
    h_send,
    h_recv,
    f_send,
    f_recv,
    g_send,
    g_recv,
):
    slots, rows, nodes = inv.shape
    ports = port_nodes.shape[1]
    scens = hist.shape[1]
    iface = slots * ports
    depth = hist.shape[0]
    width = 2 * iface
    part = rows // SPLIT
    me = lax.axis_index("scen")
    dev = lax.axis_index("sub")
    sib = me + 1 - 2 * lax.rem(me, 2)
    across = lax.rem(me + 2, 4)
    diag = 3 - me
    right = lax.rem(dev + 1, n_sub)
    left = lax.rem(dev + n_sub - 1, n_sub)

    own_copy = pltpu.make_async_copy(inv, full.at[:, pl.ds(me * rows, rows), :], own_sem)
    own_copy.start()
    state_copy = pltpu.make_async_copy(node_state, state_in, state_sem)
    state_copy.start()

    barrier = pltpu.get_barrier_semaphore()
    for peer in (across, sib, diag):
        pl.semaphore_signal(barrier, inc=1, device_id={"scen": peer}, device_id_type=MESH)

    def greet(offset, carry):
        pl.semaphore_signal(
            barrier,
            inc=1,
            device_id={"sub": lax.rem(dev + offset, n_sub)},
            device_id_type=MESH,
        )
        return carry

    lax.fori_loop(1, n_sub, greet, 0)
    pl.semaphore_wait(barrier, n_sub + 2)

    def remote(src, dst, send, recv, peer):
        return pltpu.make_async_remote_copy(
            src_ref=src,
            dst_ref=dst,
            send_sem=send,
            recv_sem=recv,
            device_id=peer,
            device_id_type=MESH,
        )

    def block(g, owner, piece):
        return full.at[g, pl.ds(owner * rows + piece * part, part), :]

    def weight_send(which, peer, g, piece):
        return remote(
            inv.at[g, pl.ds(piece * part, part), :],
            block(g, me, piece),
            w_send.at[which, g, piece],
            w_recv.at[which, g, piece],
            {"scen": peer},
        )

    def forward(g, piece):
        return remote(
            block(g, across, piece),
            block(g, across, piece),
            w_send.at[2, g, piece],
            w_recv.at[2, g, piece],
            {"scen": sib},
        )

    def forwarded(g, piece):
        return remote(
            block(g, diag, piece),
            block(g, diag, piece),
            w_send.at[2, g, piece],
            w_recv.at[2, g, piece],
            {"scen": sib},
        )

    def send_slot(g, carry):
        for piece in range(SPLIT):
            weight_send(0, across, g, piece).start()
        for piece in range(SPLIT):
            weight_send(1, sib, g, piece).start()
        return carry

    weight_send(0, across, 0, 0).start()

    def hist_send(side, peer):
        return remote(hist, hbuf.at[side], h_send.at[side], h_recv.at[side], {"sub": peer})

    hist_send(0, right).start()
    hist_send(1, left).start()

    def column(row, count):
        eye = lax.broadcasted_iota(jnp.int32, (count, count), 0) == lax.broadcasted_iota(
            jnp.int32, (count, count), 1
        )
        return jnp.sum(jnp.where(eye, row, jnp.zeros_like(row)), axis=1, keepdims=True)

    node_row = lax.broadcasted_iota(jnp.int32, (1, nodes), 1)
    hots = []
    for g in range(slots):
        col = column(port_nodes[g : g + 1, :].astype(F32), ports)
        hots.append((col == node_row.astype(F32)).astype(F32))
    hot_all = jnp.concatenate(hots, axis=0)
    slot_col = lax.broadcasted_iota(jnp.int32, (iface, 1), 0) // ports
    for g in range(slots):
        lhs[g, scens:, :] = (hot_all * (slot_col == g).astype(F32)).astype(BF16)
    hot_all = hot_all.astype(BF16)

    own_copy.wait()

    def own_cols(g, total):
        return total + dot_t(lhs[g, scens:, :], full[g, pl.ds(me * rows, rows), :])

    cols = lax.fori_loop(0, slots, own_cols, jnp.zeros((iface, rows), F32))
    my_cols = pct.at[:, pl.ds(pl.multiple_of(me * rows, rows), rows)]
    my_cols[...] = cols.astype(BF16)

    def pc_copy(which, owner, peer):
        cols_ref = pct.at[:, pl.ds(pl.multiple_of(owner * rows, rows), rows)]
        return remote(cols_ref, cols_ref, pc_send.at[which], pc_recv.at[which], {"scen": peer})

    for which, peer in enumerate((across, sib, diag)):
        pc_copy(which, me, peer).start()
    for piece in range(1, SPLIT):
        weight_send(0, across, 0, piece).start()
    for piece in range(SPLIT):
        weight_send(1, sib, 0, piece).start()
    lax.fori_loop(1, slots, send_slot, 0)

    used_row = (
        lax.broadcasted_iota(jnp.int32, (1, iface), 1) // ports < turbine_count[0]
    ).astype(F32)
    stroke_col = column(stroke_node[...].astype(F32), scens)
    amp_col = column(stroke_amp[...], scens)
    port_lane = lax.broadcasted_iota(jnp.int32, (1, iface), 1)
    partner_row = partner[...]
    delay_row = delay[...]
    paired = (partner_row != port_lane + dev * iface).astype(F32)
    port_sub = lax.broadcasted_iota(jnp.int32, (iface, 1), 0)
    picks = [
        (partner_row == port_sub + (dev + shift) * iface).astype(F32) * paired
        for shift in (-1, 0, 1)
    ]

    def pick(blocks, lag):
        chosen = (delay_row == lag).astype(F32)
        return sum(dot(b, (m * chosen).astype(BF16)) for b, m in zip(blocks, picks))

    for o in range(n_sub):
        piece = schur[:, o * iface : (o + 1) * iface]
        sbuf[:, o * width : (o + 1) * width] = jnp.concatenate([piece, piece], axis=1)

    def used(g):
        return jnp.where(g < turbine_count[0], 1.0, 0.0).astype(F32)

    def inject(k, g, current, cable_half):
        strike = amp_col * (math.exp(-0.3 * k) - math.exp(-2.0 * k))
        ids = (node_row + (dev * slots + g) * nodes).astype(F32)
        struck = jnp.where(stroke_col == ids, strike, 0.0)
        value = used(g) * (current + struck + dot(cable_half, lhs[g, scens:, :]))
        lhs[g, :scens, :] = value.astype(BF16)

    def share(k, value):
        high = value.astype(BF16)
        low = (value - high.astype(F32)).astype(BF16)
        mine = gbuf.at[k - 1, :, pl.ds(pl.multiple_of(dev * width, width), width)]
        mine[...] = jnp.concatenate([high, low], axis=1)

        def one(offset, carry):
            share_copy(k, offset, dev, lax.rem(dev + offset, n_sub)).start()
            return carry

        lax.fori_loop(1, n_sub, one, 0)

    def share_copy(k, offset, owner, peer):
        ref = gbuf.at[k - 1, :, pl.ds(pl.multiple_of(owner * width, width), width)]
        return remote(ref, ref, g_send.at[k - 1, offset], g_recv.at[k - 1, offset], {"sub": peer})

    def link(k):
        def one(offset, carry):
            owner = lax.rem(dev + n_sub - offset, n_sub)
            share_copy(k, offset, owner, owner).wait_recv()
            return carry

        lax.fori_loop(1, n_sub, one, 0)
        return dot_t(gbuf[k - 1], sbuf[...]).astype(BF16)

    state_copy.wait()
    for g in range(slots):
        companion[g] = state_in[:, g, :]
    hist_send(0, left).wait_recv()
    hist_send(1, right).wait_recv()

    def past(k):
        total = jnp.zeros((scens, iface), F32)
        for back in range(depth):
            total = total + pick((hbuf[0, back], hist[back], hbuf[1, back]), k + back)
        return total

    cable_1 = -past(1)
    cable_2 = -past(2)
    cable_3 = past(3)
    cable_half = cable_1.astype(BF16)

    def start_step(g, carry):
        inject(1, g, companion[g], cable_half)
        return carry

    lax.fori_loop(0, slots, start_step, 0)
    for which, peer in enumerate((across, sib, diag)):
        pc_copy(which, peer, peer).wait_recv()
    columns = pct[...]
    for g in range(slots):
        pcb[g] = columns * (slot_col == g).astype(BF16)
    port_slot = lax.broadcasted_iota(jnp.int32, (1, iface), 1) // ports
    port_port = (dot_t(hot_all, columns) * (slot_col == port_slot).astype(F32)).astype(BF16)

    def open_ports(g, total):
        return total + dot_t(lhs[g, :scens, :], pcb[g])

    zero_ports = jnp.zeros((scens, iface), F32)
    port_1 = lax.fori_loop(0, slots, open_ports, zero_ports)
    share(1, port_1)

    def waves(k, port_open, half, cable):
        port_volt = used_row * (port_open - dot(half, port_port))
        outgoing = (used_row * (0.5 * port_volt + cable)).astype(BF16)
        wave_out[k - 1] = outgoing
        return outgoing

    half_1 = link(1)
    fbuf[2] = waves(1, port_1, half_1, cable_1)

    def fresh_send(side, peer):
        return remote(
            fbuf.at[2], fbuf.at[side], f_send.at[side], f_recv.at[side], {"sub": peer}
        )

    fresh_send(0, right).start()
    fresh_send(1, left).start()
    cable_half_2 = cable_2.astype(BF16)

    def voltage(g, value, half):
        return used(g) * (value - dot(half, prow[g]))

    def second(g, total):
        for piece in range(SPLIT):
            weight_send(0, across, g, piece).wait_recv()
            forward(g, piece).start()
        for piece in range(SPLIT):
            weight_send(1, sib, g, piece).wait_recv()
        for piece in range(SPLIT):
            forwarded(g, piece).wait_recv()
        both = dot(lhs[g], full[g])
        prow[g] = both[scens:].astype(BF16)
        volt = voltage(g, both[:scens], half_1)
        now = -companion[g] - 2.0 * gain[pl.ds(g, 1), :] * volt
        companion[g] = now
        inject(2, g, now, cable_half_2)
        return open_ports(g, total)

    port_2 = lax.fori_loop(0, slots, second, zero_ports)
    share(2, port_2)

    def multiply(g, carry):
        opened[g] = dot(lhs[g, :scens, :], full[g])
        return carry

    lax.fori_loop(0, slots, multiply, 0)
    fresh_send(0, left).wait_recv()
    fresh_send(1, right).wait_recv()
    cable_3 = -(cable_3 + pick((fbuf[0], fbuf[2], fbuf[1]), 2))
    cable_half_3 = cable_3.astype(BF16)
    half_2 = link(2)

    def third(g, total):
        volt = voltage(g, opened[g], half_2)
        now = -companion[g] - 2.0 * gain[pl.ds(g, 1), :] * volt
        inject(3, g, now, cable_half_3)
        return open_ports(g, total)

    port_3 = lax.fori_loop(0, slots, third, zero_ports)
    share(3, port_3)
    waves(2, port_2, half_2, cable_2)
    lax.fori_loop(0, slots, multiply, 0)
    half_3 = link(3)
    waves(3, port_3, half_3, cable_3)

    def finish(g, carry):
        volt_out[g] = voltage(g, opened[g], half_3).astype(BF16)
        return carry

    lax.fori_loop(0, slots, finish, 0)

    def drain_slot(g, carry):
        for piece in range(SPLIT):
            weight_send(0, across, g, piece).wait_send()
            weight_send(1, sib, g, piece).wait_send()
            forward(g, piece).wait_send()
        return carry

    lax.fori_loop(0, slots, drain_slot, 0)
    for which, peer in enumerate((across, sib, diag)):
        pc_copy(which, me, peer).wait_send()
    for side, peer in ((0, right), (1, left)):
        hist_send(side, peer).wait_send()
        fresh_send(side, peer).wait_send()

    for k in range(1, STEPS + 1):

        def drain(offset, carry, k=k):
            share_copy(k, offset, dev, lax.rem(dev + offset, n_sub)).wait_send()
            return carry

        lax.fori_loop(1, n_sub, drain, 0)


def per_device(
    n_sub,
    internal_inverse,
    schur_inverse,
    port_nodes,
    turbine_count,
    partner_port,
    cable_delay,
    history_w,
    node_state,
    node_gain,
    stroke_node,
    stroke_amp,
):
    slots, rows, nodes = internal_inverse.shape
    ports = port_nodes.shape[1]
    scens = node_state.shape[0]
    depth = history_w.shape[0]
    iface = slots * ports
    vmem = pl.BlockSpec(memory_space=pltpu.VMEM)
    smem = pl.BlockSpec(memory_space=pltpu.SMEM)
    hbm = pl.BlockSpec(memory_space=pl.ANY)
    dma = pltpu.SemaphoreType.DMA
    volt, wave = pl.pallas_call(
        functools.partial(kernel, n_sub),
        out_shape=(
            jax.ShapeDtypeStruct((slots, scens, nodes), BF16),
            jax.ShapeDtypeStruct((STEPS, scens, iface), BF16),
        ),
        in_specs=[hbm, vmem, vmem, smem, vmem, vmem, vmem, hbm, vmem, vmem, vmem],
        out_specs=(vmem, vmem),
        scratch_shapes=[
            pltpu.VMEM((slots, nodes, nodes), BF16),
            pltpu.VMEM((scens, slots, nodes), F32),
            pltpu.VMEM((slots, scens, nodes), F32),
            pltpu.VMEM((slots, scens, nodes), F32),
            pltpu.VMEM((slots, scens + iface, nodes), BF16),
            pltpu.VMEM((slots, iface, nodes), BF16),
            pltpu.VMEM((iface, nodes), BF16),
            pltpu.VMEM((slots, iface, nodes), BF16),
            pltpu.VMEM((STEPS, scens, n_sub * 2 * iface), BF16),
            pltpu.VMEM((iface, n_sub * 2 * iface), BF16),
            pltpu.VMEM((2, depth, scens, iface), BF16),
            pltpu.VMEM((3, scens, iface), BF16),
            dma(()),
            dma(()),
            dma((3, slots, SPLIT)),
            dma((3, slots, SPLIT)),
            dma((3,)),
            dma((3,)),
            dma((2,)),
            dma((2,)),
            dma((2,)),
            dma((2,)),
            dma((STEPS, n_sub)),
            dma((STEPS, n_sub)),
        ],
        compiler_params=pltpu.CompilerParams(
            collective_id=0, has_side_effects=True, vmem_limit_bytes=60 * 1024 * 1024
        ),
        name="transient",
    )(
        internal_inverse,
        schur_inverse,
        port_nodes,
        turbine_count,
        partner_port.reshape(1, iface),
        cable_delay.reshape(1, iface),
        history_w,
        node_state,
        node_gain,
        stroke_node.reshape(1, scens),
        stroke_amp.reshape(1, scens),
    )
    return jnp.swapaxes(volt, 0, 1), wave


def solution(mesh):
    return jax.shard_map(
        functools.partial(per_device, mesh.shape["sub"]),
        mesh=mesh,
        in_specs=(
            P("sub", "scen", None),
            P("sub", None),
            P("sub", None),
            P("sub"),
            P("sub"),
            P("sub"),
            P(None, "scen", "sub"),
            P("scen", "sub", None),
            P("sub", None),
            P("scen"),
            P("scen"),
        ),
        out_specs=(P("scen", "sub", None), P(None, "scen", "sub")),
        check_vma=False,
    )
```

```python
import functools
import math

import jax
import jax.numpy as jnp
from jax import lax
from jax.experimental import pallas as pl
from jax.experimental.pallas import tpu as pltpu
from jax.sharding import PartitionSpec as P

STEPS = 3
SPLIT = 4
F32 = jnp.float32
BF16 = jnp.bfloat16
MESH = pl.DeviceIdType.MESH


def dot(left, right):
    return jnp.dot(left, right, preferred_element_type=F32)


def dot_t(left, right):
    return lax.dot_general(left, right, (((1,), (1,)), ((), ())), preferred_element_type=F32)


def kernel(
    n_sub,
    inv,
    schur_hbm,
    port_nodes_hbm,
    turbine_count_hbm,
    partner_hbm,
    delay_hbm,
    hist_hbm,
    node_state,
    gain_hbm,
    stroke_node_hbm,
    stroke_amp_hbm,
    volt_out,
    wave_out,
    full,
    state_in,
    schur,
    port_nodes,
    turbine_count,
    partner,
    delay,
    hist,
    gain,
    stroke_node,
    stroke_amp,
    companion,
    opened,
    steady,
    lhs,
    prow,
    pct,
    pcb,
    gbuf,
    sbuf,
    hbuf,
    fbuf,
    own_sem,
    state_sem,
    in_sem,
    w_send,
    w_recv,
    pc_send,
    pc_recv,
    h_send,
    h_recv,
    f_send,
    f_recv,
    g_send,
    g_recv,
):
    slots, rows, nodes = inv.shape
    ports = port_nodes.shape[1]
    scens = hist.shape[1]
    iface = slots * ports
    depth = hist.shape[0]
    width = 2 * iface
    part = rows // SPLIT
    me = lax.axis_index("scen")
    dev = lax.axis_index("sub")
    sib = me + 1 - 2 * lax.rem(me, 2)
    across = lax.rem(me + 2, 4)
    diag = 3 - me
    right = lax.rem(dev + 1, n_sub)
    left = lax.rem(dev + n_sub - 1, n_sub)

    barrier = pltpu.get_barrier_semaphore()
    for peer in (across, sib, diag):
        pl.semaphore_signal(barrier, inc=1, device_id={"scen": peer}, device_id_type=MESH)

    def greet(offset, carry):
        pl.semaphore_signal(
            barrier,
            inc=1,
            device_id={"sub": lax.rem(dev + offset, n_sub)},
            device_id_type=MESH,
        )
        return carry

    lax.fori_loop(1, n_sub, greet, 0)
    own_copy = pltpu.make_async_copy(inv, full.at[:, pl.ds(me * rows, rows), :], own_sem)
    own_copy.start()
    state_copy = pltpu.make_async_copy(node_state, state_in, state_sem)
    state_copy.start()

    small = [
        pltpu.make_async_copy(src, dst, in_sem.at[i])
        for i, (src, dst) in enumerate(
            (
                (port_nodes_hbm, port_nodes),
                (hist_hbm, hist),
                (partner_hbm, partner),
                (delay_hbm, delay),
                (turbine_count_hbm, turbine_count),
                (stroke_node_hbm, stroke_node),
                (stroke_amp_hbm, stroke_amp),
                (schur_hbm, schur),
                (gain_hbm, gain),
            )
        )
    ]
    for copy in small:
        copy.start()
    pl.semaphore_wait(barrier, n_sub + 2)

    def remote(src, dst, send, recv, peer):
        return pltpu.make_async_remote_copy(
            src_ref=src,
            dst_ref=dst,
            send_sem=send,
            recv_sem=recv,
            device_id=peer,
            device_id_type=MESH,
        )

    def block(g, owner, piece):
        return full.at[g, pl.ds(owner * rows + piece * part, part), :]

    def weight_send(which, peer, g, piece):
        return remote(
            inv.at[g, pl.ds(piece * part, part), :],
            block(g, me, piece),
            w_send.at[which, g, piece],
            w_recv.at[which, g, piece],
            {"scen": peer},
        )

    def forward(g, piece):
        return remote(
            block(g, across, piece),
            block(g, across, piece),
            w_send.at[2, g, piece],
            w_recv.at[2, g, piece],
            {"scen": sib},
        )

    def forwarded(g, piece):
        return remote(
            block(g, diag, piece),
            block(g, diag, piece),
            w_send.at[2, g, piece],
            w_recv.at[2, g, piece],
            {"scen": sib},
        )

    def send_slot(g, carry):
        for piece in range(SPLIT):
            weight_send(0, across, g, piece).start()
        for piece in range(SPLIT):
            weight_send(1, sib, g, piece).start()
        return carry

    for piece in range(SPLIT // 2):
        weight_send(0, across, 0, piece).start()
    for copy in small:
        copy.wait()

    def hist_send(side, peer):
        return remote(hist, hbuf.at[side], h_send.at[side], h_recv.at[side], {"sub": peer})

    hist_send(0, right).start()
    hist_send(1, left).start()

    def column(row, count):
        eye = lax.broadcasted_iota(jnp.int32, (count, count), 0) == lax.broadcasted_iota(
            jnp.int32, (count, count), 1
        )
        return jnp.sum(jnp.where(eye, row, jnp.zeros_like(row)), axis=1, keepdims=True)

    node_row = lax.broadcasted_iota(jnp.int32, (1, nodes), 1)
    hots = []
    for g in range(slots):
        col = column(port_nodes[g : g + 1, :].astype(F32), ports)
        hots.append((col == node_row.astype(F32)).astype(F32))
    hot_all = jnp.concatenate(hots, axis=0)
    slot_col = lax.broadcasted_iota(jnp.int32, (iface, 1), 0) // ports
    for g in range(slots):
        lhs[g, scens:, :] = (hot_all * (slot_col == g).astype(F32)).astype(BF16)
    hot_all = hot_all.astype(BF16)

    own_copy.wait()

    def own_cols(g, total):
        return total + dot_t(lhs[g, scens:, :], full[g, pl.ds(me * rows, rows), :])

    cols = lax.fori_loop(0, slots, own_cols, jnp.zeros((iface, rows), F32))
    my_cols = pct.at[:, pl.ds(pl.multiple_of(me * rows, rows), rows)]
    my_cols[...] = cols.astype(BF16)

    def pc_copy(which, owner, peer):
        cols_ref = pct.at[:, pl.ds(pl.multiple_of(owner * rows, rows), rows)]
        return remote(cols_ref, cols_ref, pc_send.at[which], pc_recv.at[which], {"scen": peer})

    for which, peer in enumerate((across, sib, diag)):
        pc_copy(which, me, peer).start()
    for piece in range(SPLIT // 2, SPLIT):
        weight_send(0, across, 0, piece).start()
    for piece in range(SPLIT):
        weight_send(1, sib, 0, piece).start()
    lax.fori_loop(1, slots, send_slot, 0)

    count = turbine_count[...]
    used_row = (lax.broadcasted_iota(jnp.int32, (1, iface), 1) // ports < count).astype(F32)
    stroke_col = column(stroke_node[...].astype(F32), scens)
    amp_col = column(stroke_amp[...], scens)
    port_lane = lax.broadcasted_iota(jnp.int32, (1, iface), 1)
    partner_row = partner[...]
    delay_row = delay[...]
    paired = (partner_row != port_lane + dev * iface).astype(F32)
    port_sub = lax.broadcasted_iota(jnp.int32, (iface, 1), 0)
    picks = [
        (partner_row == port_sub + (dev + shift) * iface).astype(F32) * paired
        for shift in (-1, 0, 1)
    ]

    def pick(blocks, lag):
        chosen = (delay_row == lag).astype(F32)
        return sum(dot(b, (m * chosen).astype(BF16)) for b, m in zip(blocks, picks))

    for o in range(n_sub):
        piece = schur[:, o * iface : (o + 1) * iface]
        sbuf[:, o * width : (o + 1) * width] = jnp.concatenate([piece, piece], axis=1)

    def used(g):
        return (g < count).astype(F32)

    def sources(k, g, cable_half):
        strike = amp_col * (math.exp(-0.3 * k) - math.exp(-2.0 * k))
        ids = (node_row + (dev * slots + g) * nodes).astype(F32)
        struck = jnp.where(stroke_col == ids, strike, 0.0)
        return struck + dot(cable_half, lhs[g, scens:, :])

    def inject(k, g, current, cable_half):
        value = used(g) * (current + sources(k, g, cable_half))
        lhs[g, :scens, :] = value.astype(BF16)

    def share(k, value):
        high = value.astype(BF16)
        low = (value - high.astype(F32)).astype(BF16)
        mine = gbuf.at[k - 1, :, pl.ds(pl.multiple_of(dev * width, width), width)]
        mine[...] = jnp.concatenate([high, low], axis=1)

        def one(offset, carry):
            share_copy(k, offset, dev, lax.rem(dev + offset, n_sub)).start()
            return carry

        lax.fori_loop(1, n_sub, one, 0)

    def share_copy(k, offset, owner, peer):
        ref = gbuf.at[k - 1, :, pl.ds(pl.multiple_of(owner * width, width), width)]
        return remote(ref, ref, g_send.at[k - 1, offset], g_recv.at[k - 1, offset], {"sub": peer})

    def link(k):
        def one(offset, carry):
            owner = lax.rem(dev + n_sub - offset, n_sub)
            share_copy(k, offset, owner, owner).wait_recv()
            return carry

        lax.fori_loop(1, n_sub, one, 0)
        return dot_t(gbuf[k - 1], sbuf[...]).astype(BF16)

    state_copy.wait()
    for g in range(slots):
        companion[g] = state_in[:, g, :]
    hist_send(0, left).wait_recv()
    hist_send(1, right).wait_recv()

    def past(k):
        total = jnp.zeros((scens, iface), F32)
        for back in range(depth):
            total = total + pick((hbuf[0, back], hist[back], hbuf[1, back]), k + back)
        return total

    cable_1 = -past(1)
    cable_2 = -past(2)
    cable_3 = past(3)
    cable_half = cable_1.astype(BF16)

    def start_step(g, carry):
        inject(1, g, companion[g], cable_half)
        return carry

    lax.fori_loop(0, slots, start_step, 0)
    for which, peer in enumerate((across, sib, diag)):
        pc_copy(which, peer, peer).wait_recv()
    columns = pct[...]
    for g in range(slots):
        pcb[g] = columns * (slot_col == g).astype(BF16)
    port_slot = lax.broadcasted_iota(jnp.int32, (1, iface), 1) // ports
    port_port = (dot_t(hot_all, columns) * (slot_col == port_slot).astype(F32)).astype(BF16)

    def open_ports(g, total):
        return total + dot_t(lhs[g, :scens, :], pcb[g])

    zero_ports = jnp.zeros((scens, iface), F32)
    port_1 = lax.fori_loop(0, slots, open_ports, zero_ports)
    share(1, port_1)

    def waves(k, port_open, half, cable):
        port_volt = used_row * (port_open - dot(half, port_port))
        outgoing = (used_row * (0.5 * port_volt + cable)).astype(BF16)
        wave_out[k - 1] = outgoing
        return outgoing

    half_1 = link(1)
    fbuf[2] = waves(1, port_1, half_1, cable_1)

    def fresh_send(side, peer):
        return remote(
            fbuf.at[2], fbuf.at[side], f_send.at[side], f_recv.at[side], {"sub": peer}
        )

    fresh_send(0, right).start()
    fresh_send(1, left).start()
    cable_half_2 = cable_2.astype(BF16)

    def voltage(g, value, half):
        return used(g) * (value - dot(half, prow[g]))

    def gain_used(g):
        return 2.0 * used(g) * gain[g : g + 1, :]

    def multiply(g):
        opened[g] = dot(lhs[g, :scens, :], full[g])

    def settle(g):
        multiply(g)
        steady[g] = used(g) * (
            sources(3, g, cable_half_3) - companion[g] - gain_used(g) * opened[g]
        )

    def quarter(g, owner):
        span = pl.ds(pl.multiple_of(owner * rows, rows), rows)
        return dot(lhs[g, :, span], full[g, span, :])

    port_2 = zero_ports
    for g in range(slots):
        if g == 1:
            fresh_send(0, left).wait_recv()
            fresh_send(1, right).wait_recv()
            cable_3 = -(cable_3 + pick((fbuf[0], fbuf[2], fbuf[1]), 2))
            cable_half_3 = cable_3.astype(BF16)
        if g:
            settle(g - 1)
        current = sources(2, g, cable_half_2) - companion[g]
        for piece in range(SPLIT):
            weight_send(1, sib, g, piece).wait_recv()
        both = quarter(g, me) + quarter(g, sib)
        for piece in range(SPLIT):
            weight_send(0, across, g, piece).wait_recv()
            forward(g, piece).start()
        both = both + quarter(g, across)
        for piece in range(SPLIT):
            forwarded(g, piece).wait_recv()
        both = both + quarter(g, diag)
        prow[g] = both[scens:].astype(BF16)
        fall = gain_used(g) * voltage(g, both[:scens], half_1)
        lhs[g, :scens, :] = (used(g) * (current - fall)).astype(BF16)
        companion[g] = -companion[g] - fall
        port_2 = open_ports(g, port_2)
    share(2, port_2)
    settle(slots - 1)
    half_2 = link(2)
    port_3 = zero_ports
    for g in range(slots):
        rise = used(g) * gain_used(g) * dot(half_2, prow[g])
        lhs[g, :scens, :] = (steady[g] + rise).astype(BF16)
        port_3 = open_ports(g, port_3)
    share(3, port_3)
    waves(2, port_2, half_2, cable_2)
    for g in range(slots):
        multiply(g)
    half_3 = link(3)
    for g in range(slots):
        volt_out[g] = voltage(g, opened[g], half_3).astype(BF16)
    waves(3, port_3, half_3, cable_3)

    def drain_slot(g, carry):
        for piece in range(SPLIT):
            weight_send(0, across, g, piece).wait_send()
            weight_send(1, sib, g, piece).wait_send()
            forward(g, piece).wait_send()
        return carry

    lax.fori_loop(0, slots, drain_slot, 0)
    for which, peer in enumerate((across, sib, diag)):
        pc_copy(which, me, peer).wait_send()
    for side, peer in ((0, right), (1, left)):
        hist_send(side, peer).wait_send()
        fresh_send(side, peer).wait_send()

    for k in range(1, STEPS + 1):

        def drain(offset, carry, k=k):
            share_copy(k, offset, dev, lax.rem(dev + offset, n_sub)).wait_send()
            return carry

        lax.fori_loop(1, n_sub, drain, 0)


def per_device(
    n_sub,
    internal_inverse,
    schur_inverse,
    port_nodes,
    turbine_count,
    partner_port,
    cable_delay,
    history_w,
    node_state,
    node_gain,
    stroke_node,
    stroke_amp,
):
    slots, rows, nodes = internal_inverse.shape
    ports = port_nodes.shape[1]
    scens = node_state.shape[0]
    depth = history_w.shape[0]
    iface = slots * ports
    vmem = pl.BlockSpec(memory_space=pltpu.VMEM)
    hbm = pl.BlockSpec(memory_space=pl.ANY)
    dma = pltpu.SemaphoreType.DMA
    volt, wave = pl.pallas_call(
        functools.partial(kernel, n_sub),
        out_shape=(
            jax.ShapeDtypeStruct((slots, scens, nodes), BF16),
            jax.ShapeDtypeStruct((STEPS, scens, iface), BF16),
        ),
        in_specs=[hbm] * 11,
        out_specs=(vmem, vmem),
        scratch_shapes=[
            pltpu.VMEM((slots, nodes, nodes), BF16),
            pltpu.VMEM((scens, slots, nodes), F32),
            pltpu.VMEM(schur_inverse.shape, BF16),
            pltpu.VMEM((slots, ports), jnp.int32),
            pltpu.VMEM((1, 1), jnp.int32),
            pltpu.VMEM((1, iface), jnp.int32),
            pltpu.VMEM((1, iface), jnp.int32),
            pltpu.VMEM((depth, scens, iface), BF16),
            pltpu.VMEM((slots, nodes), F32),
            pltpu.VMEM((1, scens), jnp.int32),
            pltpu.VMEM((1, scens), F32),
            pltpu.VMEM((slots, scens, nodes), F32),
            pltpu.VMEM((slots, scens, nodes), F32),
            pltpu.VMEM((slots, scens, nodes), F32),
            pltpu.VMEM((slots, scens + iface, nodes), BF16),
            pltpu.VMEM((slots, iface, nodes), BF16),
            pltpu.VMEM((iface, nodes), BF16),
            pltpu.VMEM((slots, iface, nodes), BF16),
            pltpu.VMEM((STEPS, scens, n_sub * 2 * iface), BF16),
            pltpu.VMEM((iface, n_sub * 2 * iface), BF16),
            pltpu.VMEM((2, depth, scens, iface), BF16),
            pltpu.VMEM((3, scens, iface), BF16),
            dma(()),
            dma(()),
            dma((9,)),
            dma((3, slots, SPLIT)),
            dma((3, slots, SPLIT)),
            dma((3,)),
            dma((3,)),
            dma((2,)),
            dma((2,)),
            dma((2,)),
            dma((2,)),
            dma((STEPS, n_sub)),
            dma((STEPS, n_sub)),
        ],
        compiler_params=pltpu.CompilerParams(
            collective_id=0, has_side_effects=True, vmem_limit_bytes=60 * 1024 * 1024
        ),
        name="transient",
    )(
        internal_inverse,
        schur_inverse,
        port_nodes,
        turbine_count.reshape(1, 1),
        partner_port.reshape(1, iface),
        cable_delay.reshape(1, iface),
        history_w,
        node_state,
        node_gain,
        stroke_node.reshape(1, scens),
        stroke_amp.reshape(1, scens),
    )
    return jnp.swapaxes(volt, 0, 1), wave


def solution(mesh):
    return jax.shard_map(
        functools.partial(per_device, mesh.shape["sub"]),
        mesh=mesh,
        in_specs=(
            P("sub", "scen", None),
            P("sub", None),
            P("sub", None),
            P("sub"),
            P("sub"),
            P("sub"),
            P(None, "scen", "sub"),
            P("scen", "sub", None),
            P("sub", None),
            P("scen"),
            P("scen"),
        ),
        out_specs=(P("scen", "sub", None), P(None, "scen", "sub")),
        check_vma=False,
    )
```

```python
import functools
import math

import jax
import jax.numpy as jnp
from jax import lax
from jax.experimental import pallas as pl
from jax.experimental.pallas import tpu as pltpu
from jax.sharding import PartitionSpec as P

STEPS = 3
SPLIT = 4
F32 = jnp.float32
BF16 = jnp.bfloat16
MESH = pl.DeviceIdType.MESH


def dot(left, right):
    return jnp.dot(left, right, preferred_element_type=F32)


def dot_t(left, right):
    return lax.dot_general(left, right, (((1,), (1,)), ((), ())), preferred_element_type=F32)


def kernel(
    n_sub,
    inv,
    schur_hbm,
    port_nodes_hbm,
    turbine_count_hbm,
    partner_hbm,
    delay_hbm,
    hist_hbm,
    node_state,
    gain_hbm,
    stroke_node_hbm,
    stroke_amp_hbm,
    volt_out,
    wave_out,
    full,
    state_in,
    schur,
    port_nodes,
    turbine_count,
    partner,
    delay,
    hist,
    gain,
    stroke_node,
    stroke_amp,
    companion,
    opened,
    steady,
    lhs,
    prow,
    pct,
    pcb,
    gbuf,
    sbuf,
    hbuf,
    fbuf,
    own_sem,
    state_sem,
    in_sem,
    w_send,
    w_recv,
    pc_send,
    pc_recv,
    h_send,
    h_recv,
    f_send,
    f_recv,
    g_send,
    g_recv,
):
    slots, rows, nodes = inv.shape
    ports = port_nodes.shape[1]
    scens = hist.shape[1]
    iface = slots * ports
    depth = hist.shape[0]
    width = 2 * iface
    part = rows // SPLIT
    me = lax.axis_index("scen")
    dev = lax.axis_index("sub")
    sib = me + 1 - 2 * lax.rem(me, 2)
    across = lax.rem(me + 2, 4)
    diag = 3 - me
    right = lax.rem(dev + 1, n_sub)
    left = lax.rem(dev + n_sub - 1, n_sub)

    barrier = pltpu.get_barrier_semaphore()
    for peer in (across, sib, diag):
        pl.semaphore_signal(barrier, inc=1, device_id={"scen": peer}, device_id_type=MESH)

    def greet(offset, carry):
        pl.semaphore_signal(
            barrier,
            inc=1,
            device_id={"sub": lax.rem(dev + offset, n_sub)},
            device_id_type=MESH,
        )
        return carry

    lax.fori_loop(1, n_sub, greet, 0)
    own_copy = pltpu.make_async_copy(inv, full.at[:, pl.ds(me * rows, rows), :], own_sem)
    own_copy.start()
    state_copy = pltpu.make_async_copy(node_state, state_in, state_sem)
    state_copy.start()

    small = [
        pltpu.make_async_copy(src, dst, in_sem.at[i])
        for i, (src, dst) in enumerate(
            (
                (port_nodes_hbm, port_nodes),
                (hist_hbm, hist),
                (partner_hbm, partner),
                (delay_hbm, delay),
                (turbine_count_hbm, turbine_count),
                (stroke_node_hbm, stroke_node),
                (stroke_amp_hbm, stroke_amp),
                (schur_hbm, schur),
                (gain_hbm, gain),
            )
        )
    ]
    for copy in small:
        copy.start()
    pl.semaphore_wait(barrier, n_sub + 2)

    def remote(src, dst, send, recv, peer):
        return pltpu.make_async_remote_copy(
            src_ref=src,
            dst_ref=dst,
            send_sem=send,
            recv_sem=recv,
            device_id=peer,
            device_id_type=MESH,
        )

    def block(g, owner, piece):
        return full.at[g, pl.ds(owner * rows + piece * part, part), :]

    def weight_send(which, peer, g, piece):
        return remote(
            inv.at[g, pl.ds(piece * part, part), :],
            block(g, me, piece),
            w_send.at[which, g, piece],
            w_recv.at[which, g, piece],
            {"scen": peer},
        )

    def forward(g, piece):
        return remote(
            block(g, across, piece),
            block(g, across, piece),
            w_send.at[2, g, piece],
            w_recv.at[2, g, piece],
            {"scen": sib},
        )

    def forwarded(g, piece):
        return remote(
            block(g, diag, piece),
            block(g, diag, piece),
            w_send.at[2, g, piece],
            w_recv.at[2, g, piece],
            {"scen": sib},
        )

    def send_slot(g, carry):
        for piece in range(SPLIT):
            weight_send(0, across, g, piece).start()
        for piece in range(SPLIT):
            weight_send(1, sib, g, piece).start()
        return carry

    for piece in range(SPLIT // 2):
        weight_send(0, across, 0, piece).start()
    for copy in small:
        copy.wait()

    def hist_send(side, peer):
        return remote(hist, hbuf.at[side], h_send.at[side], h_recv.at[side], {"sub": peer})

    hist_send(0, right).start()
    hist_send(1, left).start()

    def column(row, count):
        eye = lax.broadcasted_iota(jnp.int32, (count, count), 0) == lax.broadcasted_iota(
            jnp.int32, (count, count), 1
        )
        return jnp.sum(jnp.where(eye, row, jnp.zeros_like(row)), axis=1, keepdims=True)

    node_row = lax.broadcasted_iota(jnp.int32, (1, nodes), 1)
    hots = []
    for g in range(slots):
        col = column(port_nodes[g : g + 1, :].astype(F32), ports)
        hots.append((col == node_row.astype(F32)).astype(F32))
    hot_all = jnp.concatenate(hots, axis=0)
    slot_col = lax.broadcasted_iota(jnp.int32, (iface, 1), 0) // ports
    for g in range(slots):
        lhs[g, scens:, :] = (hot_all * (slot_col == g).astype(F32)).astype(BF16)
    hot_all = hot_all.astype(BF16)

    own_copy.wait()

    def own_cols(g, total):
        return total + dot_t(lhs[g, scens:, :], full[g, pl.ds(me * rows, rows), :])

    cols = lax.fori_loop(0, slots, own_cols, jnp.zeros((iface, rows), F32))
    my_cols = pct.at[:, pl.ds(pl.multiple_of(me * rows, rows), rows)]
    my_cols[...] = cols.astype(BF16)

    def pc_copy(which, owner, peer):
        cols_ref = pct.at[:, pl.ds(pl.multiple_of(owner * rows, rows), rows)]
        return remote(cols_ref, cols_ref, pc_send.at[which], pc_recv.at[which], {"scen": peer})

    for which, peer in enumerate((across, sib, diag)):
        pc_copy(which, me, peer).start()
    for piece in range(SPLIT // 2, SPLIT):
        weight_send(0, across, 0, piece).start()
    for piece in range(SPLIT):
        weight_send(1, sib, 0, piece).start()
    lax.fori_loop(1, slots, send_slot, 0)

    count = turbine_count[0]
    used_row = (lax.broadcasted_iota(jnp.int32, (1, iface), 1) // ports < count).astype(F32)
    stroke_col = column(stroke_node[...].astype(F32), scens)
    amp_col = column(stroke_amp[...], scens)
    port_lane = lax.broadcasted_iota(jnp.int32, (1, iface), 1)
    partner_row = partner[...]
    delay_row = delay[...]
    paired = (partner_row != port_lane + dev * iface).astype(F32)
    port_sub = lax.broadcasted_iota(jnp.int32, (iface, 1), 0)
    picks = [
        (partner_row == port_sub + (dev + shift) * iface).astype(F32) * paired
        for shift in (-1, 0, 1)
    ]

    def pick(blocks, lag):
        chosen = (delay_row == lag).astype(F32)
        return sum(dot(b, (m * chosen).astype(BF16)) for b, m in zip(blocks, picks))

    for o in range(n_sub):
        piece = schur[:, o * iface : (o + 1) * iface]
        sbuf[:, o * width : (o + 1) * width] = jnp.concatenate([piece, piece], axis=1)

    def used(g):
        return jnp.where(g < count, 1.0, 0.0).astype(F32)

    def sources(k, g, cable_half):
        strike = amp_col * (math.exp(-0.3 * k) - math.exp(-2.0 * k))
        ids = (node_row + (dev * slots + g) * nodes).astype(F32)
        struck = jnp.where(stroke_col == ids, strike, 0.0)
        return struck + dot(cable_half, lhs[g, scens:, :])

    def inject(k, g, current, cable_half):
        value = used(g) * (current + sources(k, g, cable_half))
        lhs[g, :scens, :] = value.astype(BF16)

    def share(k, value):
        high = value.astype(BF16)
        low = (value - high.astype(F32)).astype(BF16)
        mine = gbuf.at[k - 1, :, pl.ds(pl.multiple_of(dev * width, width), width)]
        mine[...] = jnp.concatenate([high, low], axis=1)

        def one(offset, carry):
            share_copy(k, offset, dev, lax.rem(dev + offset, n_sub)).start()
            return carry

        lax.fori_loop(1, n_sub, one, 0)

    def share_copy(k, offset, owner, peer):
        ref = gbuf.at[k - 1, :, pl.ds(pl.multiple_of(owner * width, width), width)]
        return remote(ref, ref, g_send.at[k - 1, offset], g_recv.at[k - 1, offset], {"sub": peer})

    def link(k):
        def one(offset, carry):
            owner = lax.rem(dev + n_sub - offset, n_sub)
            share_copy(k, offset, owner, owner).wait_recv()
            return carry

        lax.fori_loop(1, n_sub, one, 0)
        return dot_t(gbuf[k - 1], sbuf[...]).astype(BF16)

    state_copy.wait()
    for g in range(slots):
        companion[g] = state_in[:, g, :]
    hist_send(0, left).wait_recv()
    hist_send(1, right).wait_recv()

    def past(k):
        total = jnp.zeros((scens, iface), F32)
        for back in range(depth):
            total = total + pick((hbuf[0, back], hist[back], hbuf[1, back]), k + back)
        return total

    cable_1 = -past(1)
    cable_2 = -past(2)
    cable_3 = past(3)
    cable_half = cable_1.astype(BF16)

    def start_step(g, carry):
        inject(1, g, companion[g], cable_half)
        return carry

    lax.fori_loop(0, slots, start_step, 0)
    for which, peer in enumerate((across, sib, diag)):
        pc_copy(which, peer, peer).wait_recv()
    columns = pct[...]
    for g in range(slots):
        pcb[g] = columns * (slot_col == g).astype(BF16)
    port_slot = lax.broadcasted_iota(jnp.int32, (1, iface), 1) // ports
    port_port = (dot_t(hot_all, columns) * (slot_col == port_slot).astype(F32)).astype(BF16)

    def open_ports(g, total):
        return total + dot_t(lhs[g, :scens, :], pcb[g])

    zero_ports = jnp.zeros((scens, iface), F32)
    port_1 = lax.fori_loop(0, slots, open_ports, zero_ports)
    share(1, port_1)

    def waves(k, port_open, half, cable):
        port_volt = used_row * (port_open - dot(half, port_port))
        outgoing = (used_row * (0.5 * port_volt + cable)).astype(BF16)
        wave_out[k - 1] = outgoing
        return outgoing

    half_1 = link(1)
    fbuf[2] = waves(1, port_1, half_1, cable_1)

    def fresh_send(side, peer):
        return remote(
            fbuf.at[2], fbuf.at[side], f_send.at[side], f_recv.at[side], {"sub": peer}
        )

    fresh_send(0, right).start()
    fresh_send(1, left).start()
    cable_half_2 = cable_2.astype(BF16)

    def voltage(g, value, half):
        return used(g) * (value - dot(half, prow[g]))

    def gain_used(g):
        return 2.0 * used(g) * gain[g : g + 1, :]

    def multiply(g):
        opened[g] = dot(lhs[g, :scens, :], full[g])

    def settle(g):
        multiply(g)
        steady[g] = used(g) * (
            sources(3, g, cable_half_3) - companion[g] - gain_used(g) * opened[g]
        )

    def quarter(g, owner):
        span = pl.ds(pl.multiple_of(owner * rows, rows), rows)
        return dot(lhs[g, :, span], full[g, span, :])

    port_2 = zero_ports
    for g in range(slots):
        if g == 1:
            fresh_send(0, left).wait_recv()
            fresh_send(1, right).wait_recv()
            cable_3 = -(cable_3 + pick((fbuf[0], fbuf[2], fbuf[1]), 2))
            cable_half_3 = cable_3.astype(BF16)
        if g:
            settle(g - 1)
        current = sources(2, g, cable_half_2) - companion[g]
        for piece in range(SPLIT):
            weight_send(1, sib, g, piece).wait_recv()
        both = quarter(g, me) + quarter(g, sib)
        for piece in range(SPLIT):
            weight_send(0, across, g, piece).wait_recv()
            forward(g, piece).start()
        both = both + quarter(g, across)
        for piece in range(SPLIT):
            forwarded(g, piece).wait_recv()
        both = both + quarter(g, diag)
        prow[g] = both[scens:].astype(BF16)
        fall = gain_used(g) * voltage(g, both[:scens], half_1)
        lhs[g, :scens, :] = (used(g) * (current - fall)).astype(BF16)
        companion[g] = -companion[g] - fall
        port_2 = open_ports(g, port_2)
    share(2, port_2)
    settle(slots - 1)
    half_2 = link(2)
    port_3 = zero_ports
    for g in range(slots):
        rise = used(g) * gain_used(g) * dot(half_2, prow[g])
        lhs[g, :scens, :] = (steady[g] + rise).astype(BF16)
        port_3 = open_ports(g, port_3)
    share(3, port_3)
    waves(2, port_2, half_2, cable_2)
    for g in range(slots):
        multiply(g)
    half_3 = link(3)
    for g in range(slots):
        volt_out[g] = voltage(g, opened[g], half_3).astype(BF16)
    waves(3, port_3, half_3, cable_3)

    def drain_slot(g, carry):
        for piece in range(SPLIT):
            weight_send(0, across, g, piece).wait_send()
            weight_send(1, sib, g, piece).wait_send()
            forward(g, piece).wait_send()
        return carry

    lax.fori_loop(0, slots, drain_slot, 0)
    for which, peer in enumerate((across, sib, diag)):
        pc_copy(which, me, peer).wait_send()
    for side, peer in ((0, right), (1, left)):
        hist_send(side, peer).wait_send()
        fresh_send(side, peer).wait_send()

    for k in range(1, STEPS + 1):

        def drain(offset, carry, k=k):
            share_copy(k, offset, dev, lax.rem(dev + offset, n_sub)).wait_send()
            return carry

        lax.fori_loop(1, n_sub, drain, 0)


def per_device(
    n_sub,
    internal_inverse,
    schur_inverse,
    port_nodes,
    turbine_count,
    partner_port,
    cable_delay,
    history_w,
    node_state,
    node_gain,
    stroke_node,
    stroke_amp,
):
    slots, rows, nodes = internal_inverse.shape
    ports = port_nodes.shape[1]
    scens = node_state.shape[0]
    depth = history_w.shape[0]
    iface = slots * ports
    vmem = pl.BlockSpec(memory_space=pltpu.VMEM)
    hbm = pl.BlockSpec(memory_space=pl.ANY)
    dma = pltpu.SemaphoreType.DMA
    volt, wave = pl.pallas_call(
        functools.partial(kernel, n_sub),
        out_shape=(
            pltpu.VMEM((slots, scens, nodes), BF16),
            pltpu.VMEM((STEPS, scens, iface), BF16),
        ),
        in_specs=[hbm] * 11,
        out_specs=(vmem, vmem),
        scratch_shapes=[
            pltpu.VMEM((slots, nodes, nodes), BF16),
            pltpu.VMEM((scens, slots, nodes), F32),
            pltpu.VMEM(schur_inverse.shape, BF16),
            pltpu.VMEM((slots, ports), jnp.int32),
            pltpu.SMEM((1,), jnp.int32),
            pltpu.VMEM((1, iface), jnp.int32),
            pltpu.VMEM((1, iface), jnp.int32),
            pltpu.VMEM((depth, scens, iface), BF16),
            pltpu.VMEM((slots, nodes), F32),
            pltpu.VMEM((1, scens), jnp.int32),
            pltpu.VMEM((1, scens), F32),
            pltpu.VMEM((slots, scens, nodes), F32),
            pltpu.VMEM((slots, scens, nodes), F32),
            pltpu.VMEM((slots, scens, nodes), F32),
            pltpu.VMEM((slots, scens + iface, nodes), BF16),
            pltpu.VMEM((slots, iface, nodes), BF16),
            pltpu.VMEM((iface, nodes), BF16),
            pltpu.VMEM((slots, iface, nodes), BF16),
            pltpu.VMEM((STEPS, scens, n_sub * 2 * iface), BF16),
            pltpu.VMEM((iface, n_sub * 2 * iface), BF16),
            pltpu.VMEM((2, depth, scens, iface), BF16),
            pltpu.VMEM((3, scens, iface), BF16),
            dma(()),
            dma(()),
            dma((9,)),
            dma((3, slots, SPLIT)),
            dma((3, slots, SPLIT)),
            dma((3,)),
            dma((3,)),
            dma((2,)),
            dma((2,)),
            dma((2,)),
            dma((2,)),
            dma((STEPS, n_sub)),
            dma((STEPS, n_sub)),
        ],
        compiler_params=pltpu.CompilerParams(
            collective_id=0, has_side_effects=True, vmem_limit_bytes=60 * 1024 * 1024
        ),
        name="transient",
    )(
        internal_inverse,
        schur_inverse,
        port_nodes,
        turbine_count,
        partner_port.reshape(1, iface),
        cable_delay.reshape(1, iface),
        history_w,
        node_state,
        node_gain,
        stroke_node.reshape(1, scens),
        stroke_amp.reshape(1, scens),
    )
    return jnp.swapaxes(volt, 0, 1), wave


def solution(mesh):
    return jax.shard_map(
        functools.partial(per_device, mesh.shape["sub"]),
        mesh=mesh,
        in_specs=(
            P("sub", "scen", None),
            P("sub", None),
            P("sub", None),
            P("sub"),
            P("sub"),
            P("sub"),
            P(None, "scen", "sub"),
            P("scen", "sub", None),
            P("sub", None),
            P("scen"),
            P("scen"),
        ),
        out_specs=(P("scen", "sub", None), P(None, "scen", "sub")),
        check_vma=False,
    )
```

```python
import functools
import math

import jax
import jax.numpy as jnp
from jax import lax
from jax.experimental import pallas as pl
from jax.experimental.pallas import tpu as pltpu
from jax.sharding import PartitionSpec as P

STEPS = 3
SPLIT = 2
F32 = jnp.float32
BF16 = jnp.bfloat16
MESH = pl.DeviceIdType.MESH


def dot(left, right):
    return jnp.dot(left, right, preferred_element_type=F32)


def dot_t(left, right):
    return lax.dot_general(left, right, (((1,), (1,)), ((), ())), preferred_element_type=F32)


def kernel(
    n_sub,
    inv,
    schur_hbm,
    port_nodes_hbm,
    turbine_count_hbm,
    partner_hbm,
    delay_hbm,
    hist_hbm,
    node_state,
    gain_hbm,
    stroke_node_hbm,
    stroke_amp_hbm,
    volt_out,
    wave_out,
    full,
    state_in,
    schur,
    port_nodes,
    turbine_count,
    partner,
    delay,
    hist,
    gain,
    stroke_node,
    stroke_amp,
    companion,
    opened,
    steady,
    lhs,
    prow,
    pct,
    pcb,
    gbuf,
    sbuf,
    hbuf,
    fbuf,
    own_sem,
    state_sem,
    in_sem,
    w_send,
    w_recv,
    pc_send,
    pc_recv,
    h_send,
    h_recv,
    f_send,
    f_recv,
    g_send,
    g_recv,
):
    slots, rows, nodes = inv.shape
    ports = port_nodes.shape[1]
    scens = hist.shape[1]
    iface = slots * ports
    depth = hist.shape[0]
    width = 2 * iface
    part = rows // SPLIT
    me = lax.axis_index("scen")
    dev = lax.axis_index("sub")
    sib = me + 1 - 2 * lax.rem(me, 2)
    across = lax.rem(me + 2, 4)
    diag = 3 - me
    right = lax.rem(dev + 1, n_sub)
    left = lax.rem(dev + n_sub - 1, n_sub)

    barrier = pltpu.get_barrier_semaphore()
    for peer in (across, sib, diag):
        pl.semaphore_signal(barrier, inc=1, device_id={"scen": peer}, device_id_type=MESH)

    def greet(offset, carry):
        pl.semaphore_signal(
            barrier,
            inc=1,
            device_id={"sub": lax.rem(dev + offset, n_sub)},
            device_id_type=MESH,
        )
        return carry

    lax.fori_loop(1, n_sub, greet, 0)
    own_copy = pltpu.make_async_copy(inv, full.at[:, pl.ds(me * rows, rows), :], own_sem)
    own_copy.start()
    state_copy = pltpu.make_async_copy(node_state, state_in, state_sem)
    state_copy.start()

    small = [
        pltpu.make_async_copy(src, dst, in_sem.at[i])
        for i, (src, dst) in enumerate(
            (
                (port_nodes_hbm, port_nodes),
                (hist_hbm, hist),
                (partner_hbm, partner),
                (delay_hbm, delay),
                (turbine_count_hbm, turbine_count),
                (stroke_node_hbm, stroke_node),
                (stroke_amp_hbm, stroke_amp),
                (schur_hbm, schur),
                (gain_hbm, gain),
            )
        )
    ]
    for copy in small:
        copy.start()
    pl.semaphore_wait(barrier, n_sub + 2)

    def remote(src, dst, send, recv, peer):
        return pltpu.make_async_remote_copy(
            src_ref=src,
            dst_ref=dst,
            send_sem=send,
            recv_sem=recv,
            device_id=peer,
            device_id_type=MESH,
        )

    def block(g, owner, piece):
        return full.at[g, pl.ds(owner * rows + piece * part, part), :]

    def weight_send(which, peer, g, piece):
        return remote(
            inv.at[g, pl.ds(piece * part, part), :],
            block(g, me, piece),
            w_send.at[which, g, piece],
            w_recv.at[which, g, piece],
            {"scen": peer},
        )

    def forward(g, piece):
        return remote(
            block(g, across, piece),
            block(g, across, piece),
            w_send.at[2, g, piece],
            w_recv.at[2, g, piece],
            {"scen": sib},
        )

    def forwarded(g, piece):
        return remote(
            block(g, diag, piece),
            block(g, diag, piece),
            w_send.at[2, g, piece],
            w_recv.at[2, g, piece],
            {"scen": sib},
        )

    def send_slot(g, carry):
        for piece in range(SPLIT):
            weight_send(0, across, g, piece).start()
        for piece in range(SPLIT):
            weight_send(1, sib, g, piece).start()
        return carry

    for piece in range(SPLIT // 2):
        weight_send(0, across, 0, piece).start()
    for copy in small:
        copy.wait()

    def hist_send(side, peer):
        return remote(hist, hbuf.at[side], h_send.at[side], h_recv.at[side], {"sub": peer})

    hist_send(0, right).start()
    hist_send(1, left).start()

    def column(row, count):
        eye = lax.broadcasted_iota(jnp.int32, (count, count), 0) == lax.broadcasted_iota(
            jnp.int32, (count, count), 1
        )
        return jnp.sum(jnp.where(eye, row, jnp.zeros_like(row)), axis=1, keepdims=True)

    node_row = lax.broadcasted_iota(jnp.int32, (1, nodes), 1)
    hots = []
    for g in range(slots):
        col = column(port_nodes[g : g + 1, :].astype(F32), ports)
        hots.append((col == node_row.astype(F32)).astype(F32))
    hot_all = jnp.concatenate(hots, axis=0)
    slot_col = lax.broadcasted_iota(jnp.int32, (iface, 1), 0) // ports
    for g in range(slots):
        lhs[g, scens:, :] = (hot_all * (slot_col == g).astype(F32)).astype(BF16)
    hot_all = hot_all.astype(BF16)

    own_copy.wait()

    def own_cols(g, total):
        return total + dot_t(lhs[g, scens:, :], full[g, pl.ds(me * rows, rows), :])

    cols = lax.fori_loop(0, slots, own_cols, jnp.zeros((iface, rows), F32))
    my_cols = pct.at[:, pl.ds(pl.multiple_of(me * rows, rows), rows)]
    my_cols[...] = cols.astype(BF16)

    def pc_copy(which, owner, peer):
        cols_ref = pct.at[:, pl.ds(pl.multiple_of(owner * rows, rows), rows)]
        return remote(cols_ref, cols_ref, pc_send.at[which], pc_recv.at[which], {"scen": peer})

    for which, peer in enumerate((across, sib, diag)):
        pc_copy(which, me, peer).start()
    for piece in range(SPLIT // 2, SPLIT):
        weight_send(0, across, 0, piece).start()
    for piece in range(SPLIT):
        weight_send(1, sib, 0, piece).start()
    lax.fori_loop(1, slots, send_slot, 0)

    count = turbine_count[0]
    used_row = (lax.broadcasted_iota(jnp.int32, (1, iface), 1) // ports < count).astype(F32)
    stroke_col = column(stroke_node[...].astype(F32), scens)
    amp_col = column(stroke_amp[...], scens)
    port_lane = lax.broadcasted_iota(jnp.int32, (1, iface), 1)
    partner_row = partner[...]
    delay_row = delay[...]
    paired = (partner_row != port_lane + dev * iface).astype(F32)
    port_sub = lax.broadcasted_iota(jnp.int32, (iface, 1), 0)
    picks = [
        (partner_row == port_sub + (dev + shift) * iface).astype(F32) * paired
        for shift in (-1, 0, 1)
    ]

    def pick(blocks, lag):
        chosen = (delay_row == lag).astype(F32)
        return sum(dot(b, (m * chosen).astype(BF16)) for b, m in zip(blocks, picks))

    for o in range(n_sub):
        piece = schur[:, o * iface : (o + 1) * iface]
        sbuf[:, o * width : (o + 1) * width] = jnp.concatenate([piece, piece], axis=1)

    def used(g):
        return jnp.where(g < count, 1.0, 0.0).astype(F32)

    def sources(k, g, cable_half):
        strike = amp_col * (math.exp(-0.3 * k) - math.exp(-2.0 * k))
        ids = (node_row + (dev * slots + g) * nodes).astype(F32)
        struck = jnp.where(stroke_col == ids, strike, 0.0)
        return struck + dot(cable_half, lhs[g, scens:, :])

    def inject(k, g, current, cable_half):
        value = used(g) * (current + sources(k, g, cable_half))
        lhs[g, :scens, :] = value.astype(BF16)

    def share(k, value):
        high = value.astype(BF16)
        low = (value - high.astype(F32)).astype(BF16)
        mine = gbuf.at[k - 1, :, pl.ds(pl.multiple_of(dev * width, width), width)]
        mine[...] = jnp.concatenate([high, low], axis=1)

        def one(offset, carry):
            share_copy(k, offset, dev, lax.rem(dev + offset, n_sub)).start()
            return carry

        lax.fori_loop(1, n_sub, one, 0)

    def share_copy(k, offset, owner, peer):
        ref = gbuf.at[k - 1, :, pl.ds(pl.multiple_of(owner * width, width), width)]
        return remote(ref, ref, g_send.at[k - 1, offset], g_recv.at[k - 1, offset], {"sub": peer})

    def link(k):
        def one(offset, carry):
            owner = lax.rem(dev + n_sub - offset, n_sub)
            share_copy(k, offset, owner, owner).wait_recv()
            return carry

        lax.fori_loop(1, n_sub, one, 0)
        return dot_t(gbuf[k - 1], sbuf[...]).astype(BF16)

    state_copy.wait()
    for g in range(slots):
        companion[g] = state_in[:, g, :]
    hist_send(0, left).wait_recv()
    hist_send(1, right).wait_recv()

    def past(k):
        total = jnp.zeros((scens, iface), F32)
        for back in range(depth):
            total = total + pick((hbuf[0, back], hist[back], hbuf[1, back]), k + back)
        return total

    cable_1 = -past(1)
    cable_2 = -past(2)
    cable_3 = past(3)
    cable_half = cable_1.astype(BF16)

    def start_step(g, carry):
        inject(1, g, companion[g], cable_half)
        return carry

    lax.fori_loop(0, slots, start_step, 0)
    for which, peer in enumerate((across, sib, diag)):
        pc_copy(which, peer, peer).wait_recv()
    columns = pct[...]
    for g in range(slots):
        pcb[g] = columns * (slot_col == g).astype(BF16)
    port_slot = lax.broadcasted_iota(jnp.int32, (1, iface), 1) // ports
    port_port = (dot_t(hot_all, columns) * (slot_col == port_slot).astype(F32)).astype(BF16)

    def open_ports(g, total):
        return total + dot_t(lhs[g, :scens, :], pcb[g])

    zero_ports = jnp.zeros((scens, iface), F32)
    port_1 = lax.fori_loop(0, slots, open_ports, zero_ports)
    share(1, port_1)

    def waves(k, port_open, half, cable):
        port_volt = used_row * (port_open - dot(half, port_port))
        outgoing = (used_row * (0.5 * port_volt + cable)).astype(BF16)
        wave_out[k - 1] = outgoing
        return outgoing

    half_1 = link(1)
    fbuf[2] = waves(1, port_1, half_1, cable_1)

    def fresh_send(side, peer):
        return remote(
            fbuf.at[2], fbuf.at[side], f_send.at[side], f_recv.at[side], {"sub": peer}
        )

    fresh_send(0, right).start()
    fresh_send(1, left).start()
    cable_half_2 = cable_2.astype(BF16)

    def voltage(g, value, half):
        return used(g) * (value - dot(half, prow[g]))

    def gain_used(g):
        return 2.0 * used(g) * gain[g : g + 1, :]

    def multiply(g):
        opened[g] = dot(lhs[g, :scens, :], full[g])

    def settle(g):
        multiply(g)
        steady[g] = used(g) * (
            sources(3, g, cable_half_3) - companion[g] - gain_used(g) * opened[g]
        )

    def quarter(g, owner):
        span = pl.ds(pl.multiple_of(owner * rows, rows), rows)
        return dot(lhs[g, :, span], full[g, span, :])

    port_2 = zero_ports
    for g in range(slots):
        if g == 1:
            fresh_send(0, left).wait_recv()
            fresh_send(1, right).wait_recv()
            cable_3 = -(cable_3 + pick((fbuf[0], fbuf[2], fbuf[1]), 2))
            cable_half_3 = cable_3.astype(BF16)
        if g:
            settle(g - 1)
        current = sources(2, g, cable_half_2) - companion[g]
        for piece in range(SPLIT):
            weight_send(1, sib, g, piece).wait_recv()
        both = quarter(g, me) + quarter(g, sib)
        for piece in range(SPLIT):
            weight_send(0, across, g, piece).wait_recv()
            forward(g, piece).start()
        both = both + quarter(g, across)
        for piece in range(SPLIT):
            forwarded(g, piece).wait_recv()
        both = both + quarter(g, diag)
        prow[g] = both[scens:].astype(BF16)
        fall = gain_used(g) * voltage(g, both[:scens], half_1)
        lhs[g, :scens, :] = (used(g) * (current - fall)).astype(BF16)
        companion[g] = -companion[g] - fall
        port_2 = open_ports(g, port_2)
    share(2, port_2)
    settle(slots - 1)
    half_2 = link(2)
    port_3 = zero_ports
    for g in range(slots):
        rise = used(g) * gain_used(g) * dot(half_2, prow[g])
        lhs[g, :scens, :] = (steady[g] + rise).astype(BF16)
        port_3 = open_ports(g, port_3)
    share(3, port_3)
    waves(2, port_2, half_2, cable_2)
    for g in range(slots):
        multiply(g)
    half_3 = link(3)
    for g in range(slots):
        volt_out[g] = voltage(g, opened[g], half_3).astype(BF16)
    waves(3, port_3, half_3, cable_3)

    def drain_slot(g, carry):
        for piece in range(SPLIT):
            weight_send(0, across, g, piece).wait_send()
            weight_send(1, sib, g, piece).wait_send()
            forward(g, piece).wait_send()
        return carry

    lax.fori_loop(0, slots, drain_slot, 0)
    for which, peer in enumerate((across, sib, diag)):
        pc_copy(which, me, peer).wait_send()
    for side, peer in ((0, right), (1, left)):
        hist_send(side, peer).wait_send()
        fresh_send(side, peer).wait_send()

    for k in range(1, STEPS + 1):

        def drain(offset, carry, k=k):
            share_copy(k, offset, dev, lax.rem(dev + offset, n_sub)).wait_send()
            return carry

        lax.fori_loop(1, n_sub, drain, 0)


def per_device(
    n_sub,
    internal_inverse,
    schur_inverse,
    port_nodes,
    turbine_count,
    partner_port,
    cable_delay,
    history_w,
    node_state,
    node_gain,
    stroke_node,
    stroke_amp,
):
    slots, rows, nodes = internal_inverse.shape
    ports = port_nodes.shape[1]
    scens = node_state.shape[0]
    depth = history_w.shape[0]
    iface = slots * ports
    vmem = pl.BlockSpec(memory_space=pltpu.VMEM)
    hbm = pl.BlockSpec(memory_space=pl.ANY)
    dma = pltpu.SemaphoreType.DMA
    volt, wave = pl.pallas_call(
        functools.partial(kernel, n_sub),
        out_shape=(
            pltpu.VMEM((slots, scens, nodes), BF16),
            pltpu.VMEM((STEPS, scens, iface), BF16),
        ),
        in_specs=[hbm] * 11,
        out_specs=(vmem, vmem),
        scratch_shapes=[
            pltpu.VMEM((slots, nodes, nodes), BF16),
            pltpu.VMEM((scens, slots, nodes), F32),
            pltpu.VMEM(schur_inverse.shape, BF16),
            pltpu.VMEM((slots, ports), jnp.int32),
            pltpu.SMEM((1,), jnp.int32),
            pltpu.VMEM((1, iface), jnp.int32),
            pltpu.VMEM((1, iface), jnp.int32),
            pltpu.VMEM((depth, scens, iface), BF16),
            pltpu.VMEM((slots, nodes), F32),
            pltpu.VMEM((1, scens), jnp.int32),
            pltpu.VMEM((1, scens), F32),
            pltpu.VMEM((slots, scens, nodes), F32),
            pltpu.VMEM((slots, scens, nodes), F32),
            pltpu.VMEM((slots, scens, nodes), F32),
            pltpu.VMEM((slots, scens + iface, nodes), BF16),
            pltpu.VMEM((slots, iface, nodes), BF16),
            pltpu.VMEM((iface, nodes), BF16),
            pltpu.VMEM((slots, iface, nodes), BF16),
            pltpu.VMEM((STEPS, scens, n_sub * 2 * iface), BF16),
            pltpu.VMEM((iface, n_sub * 2 * iface), BF16),
            pltpu.VMEM((2, depth, scens, iface), BF16),
            pltpu.VMEM((3, scens, iface), BF16),
            dma(()),
            dma(()),
            dma((9,)),
            dma((3, slots, SPLIT)),
            dma((3, slots, SPLIT)),
            dma((3,)),
            dma((3,)),
            dma((2,)),
            dma((2,)),
            dma((2,)),
            dma((2,)),
            dma((STEPS, n_sub)),
            dma((STEPS, n_sub)),
        ],
        compiler_params=pltpu.CompilerParams(
            collective_id=0, has_side_effects=True, vmem_limit_bytes=60 * 1024 * 1024
        ),
        name="transient",
    )(
        internal_inverse,
        schur_inverse,
        port_nodes,
        turbine_count,
        partner_port.reshape(1, iface),
        cable_delay.reshape(1, iface),
        history_w,
        node_state,
        node_gain,
        stroke_node.reshape(1, scens),
        stroke_amp.reshape(1, scens),
    )
    return jnp.swapaxes(volt, 0, 1), wave


def solution(mesh):
    return jax.shard_map(
        functools.partial(per_device, mesh.shape["sub"]),
        mesh=mesh,
        in_specs=(
            P("sub", "scen", None),
            P("sub", None),
            P("sub", None),
            P("sub"),
            P("sub"),
            P("sub"),
            P(None, "scen", "sub"),
            P("scen", "sub", None),
            P("sub", None),
            P("scen"),
            P("scen"),
        ),
        out_specs=(P("scen", "sub", None), P(None, "scen", "sub")),
        check_vma=False,
    )
```
